512 devices in a mesh: ctx: 64 (over z_hi, x, y), exp: 8 (over z_lo, core).
Axes of the slice: x: 4, y: 4, z: 16 (z_hi: 4, z_lo: 4; z = z_hi * 4 + z_lo), core: 2. Of those that a mesh axis runs over, the one named last changes fastest.
Arguments:
- queries: bfloat16 [65536, 2048], P('ctx', 'exp'), may hold values from -150 to 150
- keys: bfloat16 [65536, 2048], P('ctx', 'exp'), may hold values from -6 to 6
- values: bfloat16 [65536, 2048], P('ctx', 'exp'), may hold values from -6 to 6
- segment_ids: int32 [65536], P('ctx'), may hold values from 0 to 255, never falling along the last dimension, each value on 1 to 1024 neighbouring positions
- out_proj: bfloat16 [2048, 1280], P('exp'), may hold values from -0.125 to 0.125
- residual: bfloat16 [65536, 1280], P(('ctx', 'exp')), may hold values from -6 to 6
- norm_gain: float32 [1280], replicated, may hold values from 0.1 to 1.9
- expert_ids: int32 [65536, 6], P(('ctx', 'exp')), may hold values from 0 to 63, all different within a row; in each aligned block of 128 rows (0 to 127, 128 to 255, ...) at most 16 rows name the same one
- gate_weights: float32 [65536, 6], P(('ctx', 'exp')), may hold values from 0.05 to 0.4
- expert_up: bfloat16 [64, 768, 1280], P('ctx', 'exp'), may hold values from -0.15625 to 0.15625
- expert_down: bfloat16 [64, 768, 1280], P('ctx', 'exp'), may hold values from -0.21875 to 0.21875
Outputs:
- layer_out: bfloat16 [65536, 1280], P(('ctx', 'exp'))
The draws below stay inside these ranges and needn't reach their ends.
Inputs may be any that keep to these rules, and one draw needn't show every extreme that they name: `segment_ids`: segment ids never fall; every segment spans 1 to 1024 consecutive tokens, one exactly 1024. `expert_ids`: each row names 6 different experts. In each aligned block of 128 rows (the rows of one device) no expert is named by more than 16 rows, a bound that some block reaches.
All inputs are finite; a program needn't handle non-finite values.
Results may differ from the reference program's by a relative error of at most 0.01.
Values may be sent and summed in bfloat16 or wider, within the bound.
A program may use at most 64 MiB of HBM per device.

```python
import math
import jax
import jax.numpy as jnp
import numpy as np
from jax import lax

D = 1280
FF = 768
HEADS = 16
HEAD = 128
TOP = 6
TOK_DEV = 128
EXPERTS = 64
TOK_CTX = 1024
SEQ = 65536
SEGS = 256
CAP = 16
N_CTX = 64
N_EXP = 8
DEVICES = 512


def draw_pair(key):
    base = jax.random.fold_in(key, 7)
    key_query, key_key = jax.random.split(base, 2)
    keys_raw = jnp.clip(jax.random.normal(key_key, (SEQ, HEADS, HEAD), jnp.float32), -6.0, 6.0)
    queries_raw = jnp.clip(jax.random.normal(key_query, (SEQ, HEADS, HEAD), jnp.float32), -6.0, 6.0)
    keys_out = keys_raw
    queries_out = queries_raw
    return (queries_out.reshape(SEQ, HEADS * HEAD), keys_out.reshape(SEQ, HEADS * HEAD))


def draw_queries(key, part):
    return draw_pair(key)[0].astype(jnp.bfloat16)


def draw_keys(key, part):
    return draw_pair(key)[1].astype(jnp.bfloat16)


def steps_of(stream_key, shape, cuts, least, largest):
    gain = 1.0
    for axis_at, blocks in cuts:
        draws = jax.random.uniform(jax.random.fold_in(jax.random.fold_in(stream_key, 6), axis_at), (blocks,), jnp.float32, least / len(cuts), largest / len(cuts))
        gain = gain * jnp.repeat(jnp.exp(draws), shape[axis_at] // blocks).reshape((-1,) + (1,) * (len(shape) - 1 - axis_at))
    return gain


def profile(count, total, bound, slope):
    portions = [(1 << 20) // math.isqrt(rank ** slope) + 1 for rank in range(2, count + 1)]
    spare, given = total - bound - (count - 1), [1] * (count - 1)
    while spare > 0:
        movable = [i for i in range(count - 1) if given[i] < bound]
        mass, budget = sum([portions[i] for i in movable]), spare
        for i in movable:
            more = min(bound - given[i], max(1, budget * portions[i] // mass), spare)
            given[i] = given[i] + more
            spare = spare - more
    return np.array([bound] + given)


def ragged(stream_key, count, total, bound, lean):
    if count == 2:
        one = jax.random.randint(stream_key, (), max(1, total - bound), min(bound, total - 1) + 1)
        return jnp.stack([one, total - one])
    sizes = jnp.asarray(profile(count, total, bound, lean), jnp.int32)
    pairs = (count - 1) // 2
    donor, receiver = sizes[1:1 + 2 * pairs:2], sizes[2:2 + 2 * pairs:2]
    room = jnp.minimum(donor - 1, bound - receiver)
    moved = jax.random.randint(jax.random.fold_in(stream_key, 1), (pairs,), 0, 1 << 20) % (room + 1)
    sizes = sizes.at[1:1 + 2 * pairs:2].set(donor - moved).at[2:2 + 2 * pairs:2].set(receiver + moved)
    return sizes[jax.random.permutation(jax.random.fold_in(stream_key, 2), count)]


def assign_block(rng, own, number, rows, amount, top, reach, lean):
    order = jax.random.permutation(rng, amount)
    crowded, common = load_shares(amount, rows * top, reach, lean, True), load_shares(amount, rows * top, reach, lean, False)
    places = jnp.arange(amount)

    def named(sizes, rotation):
        used = int((sizes > 0).sum())
        fixed = max(1, used // 4)
        moved = fixed + (places - fixed + rotation * (used - fixed)) % max(1, amount - fixed)
        return jnp.zeros((amount,), jnp.int32).at[order[jnp.where(places < fixed, places, moved)]].set(jnp.asarray(sizes, jnp.int32))

    sizes = jnp.where(number % 4 == 0, named(crowded, number // 4), named(common, number - number // 4 - 1))
    mixed = jax.random.permutation(jax.random.fold_in(own, 3), amount)
    donor, sink = mixed[0:amount // 2 * 2:2], mixed[1:amount // 2 * 2:2]
    slack = jnp.minimum(sizes[donor] - 1, reach - sizes[sink]) // 2
    slack = jnp.where((donor == order[0]) | (sink == order[0]) | (sizes[sink] == 0), 0, jnp.maximum(slack, 0))
    moved = jax.random.randint(jax.random.fold_in(own, 4), (amount // 2,), 0, 1 << 20) % (slack + 1)
    sizes = sizes.at[donor].add(-moved).at[sink].add(moved)
    items = jnp.searchsorted(jnp.cumsum(sizes), jnp.arange(rows * top), side="right").astype(jnp.int32)
    grid = items.reshape(top, rows).T
    grid = grid[jax.random.permutation(jax.random.fold_in(own, 1), rows)]
    rotation = jax.random.randint(jax.random.fold_in(own, 2), (rows, 1), 0, top)
    return jnp.take_along_axis(grid, (jnp.arange(top)[None, :] + rotation) % top, axis=1)


def load_shares(amount, total, reach, skew, full):
    loads = [(1 << 20) // math.isqrt(grade ** skew) + 1 for grade in range(1, amount + 1)]
    largest = reach if full else min(reach, max(-(-total // amount), total * loads[0] // sum(loads)))
    least = 1 if total - largest >= amount - 1 else 0
    counts, rest = [largest] + [least] * (amount - 1), total - largest - least * (amount - 1)
    while rest > 0:
        movable = [i for i in range(1, amount) if counts[i] < largest] or [i for i in range(1, amount) if counts[i] < reach]
        mass, budget = sum([loads[i] for i in movable]), rest
        for i in movable:
            more = min(reach - counts[i], max(1, budget * loads[i] // mass), rest)
            counts[i] = counts[i] + more
            rest = rest - more
    return np.array(counts)


def scatter_about(rng, shape, spread, most, cuts=(), kind=jnp.bfloat16):
    level = steps_of(rng, shape, cuts, -0.22, 0.18) if cuts else 1.0
    values = jax.random.normal(rng, shape, jnp.float32) * spread * level
    return jnp.minimum(jnp.maximum(values, -most), most).astype(kind)


def setup_inputs(seed: int = 0) -> dict:
    key_of = jax.random.split(jax.random.key(seed), 12)
    queries = draw_queries(jax.random.fold_in(key_of[11], 71), 0)
    keys = draw_keys(jax.random.fold_in(key_of[11], 71), 0)
    values = scatter_about(key_of[2], (SEQ, HEADS * HEAD), 1.0, 6.0, ((0, 64), (1, 8)))
    segment_ids = jnp.searchsorted(jnp.cumsum(ragged(key_of[3], SEGS, SEQ, TOK_CTX, 1)), jnp.arange(SEQ), side="right").astype(jnp.int32)
    out_proj = scatter_about(key_of[4], (HEADS * HEAD, D), (HEADS * HEAD) ** -0.5, 0.125, ((0, 8),))
    residual = scatter_about(key_of[5], (SEQ, D), 1.0, 6.0, ((0, 512),))
    norm_gain = jnp.clip(1.0 + 0.18 * jax.random.normal(key_of[6], (D,), jnp.float32), 0.1, 1.9)
    expert_ids_keys = jax.random.split(jax.random.fold_in(key_of[7], 1), SEQ // TOK_DEV)
    expert_ids_turns = jax.random.permutation(jax.random.fold_in(key_of[7], 3), SEQ // TOK_DEV)
    expert_ids = jax.vmap(lambda own, number: assign_block(jax.random.fold_in(key_of[7], 2), own, number, TOK_DEV, EXPERTS, TOP, CAP, 2))(expert_ids_keys, expert_ids_turns).reshape((SEQ, TOP))
    gate_weights = jnp.clip(0.05 + 0.35 * jax.random.uniform(key_of[8], (SEQ, TOP), jnp.float32) ** steps_of(key_of[8], (SEQ, TOP), ((0, 512),), -0.2, 0.2), 0.05, 0.4)
    expert_up = scatter_about(key_of[9], (EXPERTS, FF, D), D ** -0.5, 0.15625, ((0, 64), (1, 8)))
    expert_down = scatter_about(key_of[10], (EXPERTS, FF, D), FF ** -0.5, 0.21875, ((0, 64), (1, 8)))
    return dict(queries=queries, keys=keys, values=values, segment_ids=segment_ids, out_proj=out_proj, residual=residual, norm_gain=norm_gain, expert_ids=expert_ids, gate_weights=gate_weights, expert_up=expert_up, expert_down=expert_down)


def attend(query_rows, key_rows, value_rows, allowed):
    scores = jnp.einsum('qhd,khd->hqk', query_rows.astype(jnp.float32), key_rows.astype(jnp.float32)) * HEAD ** (-0.5)
    row_max = lax.optimization_barrier(jnp.max(jnp.where(allowed[None], scores, -1e+30), axis=2, keepdims=True))
    weights = jnp.exp(jnp.where(allowed[None], scores - row_max, -jnp.inf))
    probabilities = (weights / lax.optimization_barrier(jnp.sum(weights, axis=2, keepdims=True))).astype(jnp.bfloat16)
    return jnp.einsum('hqk,khd->qhd', probabilities.astype(jnp.float32), value_rows.astype(jnp.float32)).astype(jnp.bfloat16)

def reference(queries, keys, values, segment_ids, out_proj, residual, norm_gain, expert_ids, gate_weights, expert_up, expert_down):
    shard_len = TOK_DEV * N_EXP
    query_blocks = queries.reshape(N_CTX, shard_len, HEADS, HEAD)
    key_blocks = keys.reshape(N_CTX, shard_len, HEADS, HEAD)
    value_blocks = values.reshape(N_CTX, shard_len, HEADS, HEAD)
    seg_marks = (segment_ids + 1).reshape(N_CTX, shard_len)
    empty_block = jnp.zeros((1, shard_len, HEADS, HEAD), jnp.bfloat16)
    prev_keys = jnp.concatenate([empty_block, key_blocks[:-1]], axis=0)
    prev_values = jnp.concatenate([empty_block, value_blocks[:-1]], axis=0)
    prev_marks = jnp.concatenate([jnp.zeros((1, shard_len), jnp.int32), seg_marks[:-1]], axis=0)
    positions = jnp.arange(shard_len, dtype=jnp.int32)
    key_positions = jnp.concatenate([positions - shard_len, positions])

    def one_block(operands):
        query_rows, own_keys, own_values, own_marks, early_keys, early_values, early_marks = operands
        both_keys = jnp.concatenate([early_keys, own_keys], axis=0)
        both_values = jnp.concatenate([early_values, own_values], axis=0)
        both_marks = jnp.concatenate([early_marks, own_marks])
        allowed = (both_marks[None, :] == own_marks[:, None]) & (key_positions[None, :] <= positions[:, None])
        return attend(query_rows, both_keys, both_values, allowed)
    attention = lax.map(one_block, (query_blocks, key_blocks, value_blocks, seg_marks, prev_keys, prev_values, prev_marks))
    attention = attention.reshape(SEQ, HEADS * HEAD)
    group_width = HEADS * HEAD // N_EXP

    def add_group(group, running):
        columns = lax.dynamic_slice_in_dim(attention, group * group_width, group_width, 1)
        weight_rows = lax.dynamic_slice_in_dim(out_proj, group * group_width, group_width, 0)
        partial_sum = jnp.dot(columns, weight_rows, preferred_element_type=jnp.float32).astype(jnp.bfloat16)
        partial_sum = lax.optimization_barrier(partial_sum)
        return running + partial_sum.astype(jnp.float32)
    projected = lax.fori_loop(0, N_EXP, add_group, jnp.zeros((SEQ, D), jnp.float32))
    stream = (residual.astype(jnp.float32) + projected).astype(jnp.bfloat16)
    stream_f = stream.astype(jnp.float32)
    mean_square = lax.optimization_barrier(jnp.mean(stream_f * stream_f, axis=1, keepdims=True))
    normed = (stream_f * lax.rsqrt(mean_square + 1e-06) * norm_gain[None, :]).astype(jnp.bfloat16)
    most_rows = CAP * DEVICES
    flat_ids = expert_ids.reshape(-1)
    flat_gates = gate_weights.reshape(-1)
    token_of = jnp.arange(SEQ * TOP, dtype=jnp.int32) // TOP

    def one_expert(running, expert):
        matches = flat_ids == expert
        picks = jnp.nonzero(matches, size=most_rows, fill_value=0)[0].astype(jnp.int32)
        match_count = jnp.sum(matches.astype(jnp.int32))
        valid = jnp.arange(most_rows, dtype=jnp.int32) < match_count
        tokens_here = token_of[picks]
        row_block = normed[tokens_here]
        up_matrix = lax.dynamic_index_in_dim(expert_up, expert, 0, keepdims=False)
        down_matrix = lax.dynamic_index_in_dim(expert_down, expert, 0, keepdims=False)
        hidden = jax.nn.silu(jnp.dot(row_block, up_matrix.T, preferred_element_type=jnp.float32)).astype(jnp.bfloat16)
        expert_out = jnp.dot(hidden, down_matrix, preferred_element_type=jnp.float32).astype(jnp.bfloat16)
        gate_here = jnp.where(valid, flat_gates[picks], jnp.zeros((), jnp.float32))
        running = running.at[tokens_here].add(gate_here[:, None] * expert_out.astype(jnp.float32))
        return (running, None)
    mixture, _ = lax.scan(one_expert, jnp.zeros((SEQ, D), jnp.float32), jnp.arange(EXPERTS, dtype=jnp.int32))
    return (stream_f + mixture).astype(jnp.bfloat16)
```

```python
import math
import jax
import jax.numpy as jnp
from jax import lax
from jax.experimental import pallas as pl
from jax.sharding import PartitionSpec as P

HEAD = 128
TOP = 6
CAP = 16
BOTH = ("ctx", "exp")
ZH, NX, NY, ZL, NC = 4, 4, 4, 4, 2
NZ = ZH * ZL
PLANE = NX * NY


def join(z, x, y, c):
    zh, zl = z // ZL, z % ZL
    return ((zh * NX + x) * NY + y) * (ZL * NC) + zl * NC + c


def route(target):
    return [
        (join(z, x, y, c), join(*target(z, x, y, c)))
        for z in range(NZ)
        for x in range(NX)
        for y in range(NY)
        for c in range(NC)
    ]


SWAP = route(lambda z, x, y, c: (z, x, y, 1 - c))
RING = route(lambda z, x, y, c: ((z + 1 - 2 * c) % NZ, x, y, c))


def send(block, pairs):
    return lax.ppermute(block, BOTH, pairs)


def shifted(block, axis, distance):
    devices = range(lax.axis_size(axis))
    pairs = [(i - distance, i) for i in devices if i - distance in devices]
    return lax.ppermute(block, axis, pairs)


def attend(query_rows, key_rows, value_rows, query_marks, key_marks):
    shard_len, width = query_rows.shape
    block_rows = min(256, shard_len)
    span = shard_len + block_rows
    scale = HEAD ** (-0.5) * math.log2(math.e)

    def kernel(q_ref, k_ref, v_ref, mq_ref, mk_ref, out_ref):
        window = pl.ds(pl.multiple_of(pl.program_id(1) * block_rows, block_rows), span)
        scores = lax.dot_general(
            q_ref[...],
            k_ref[window, :],
            (((1,), (1,)), ((), ())),
            preferred_element_type=jnp.float32,
        )
        row = lax.broadcasted_iota(jnp.int32, (block_rows, span), 0)
        column = lax.broadcasted_iota(jnp.int32, (block_rows, span), 1)
        allowed = (mk_ref[:, window] == mq_ref[...]) & (column - row <= shard_len)
        scores = jnp.where(allowed, scores, -1e30)
        row_max = jnp.max(scores, axis=1, keepdims=True)
        weights = jnp.exp2((scores - row_max) * scale)
        total = jnp.sum(weights, axis=1, keepdims=True)
        mixed = jnp.dot(
            weights.astype(jnp.bfloat16), v_ref[window, :], preferred_element_type=jnp.float32
        )
        out_ref[...] = (mixed / total).astype(out_ref.dtype)

    keys_here = key_rows.shape[0]
    return pl.pallas_call(
        kernel,
        grid=(width // HEAD, shard_len // block_rows),
        in_specs=[
            pl.BlockSpec((block_rows, HEAD), lambda h, b: (b, h)),
            pl.BlockSpec((keys_here, HEAD), lambda h, b: (0, h)),
            pl.BlockSpec((keys_here, HEAD), lambda h, b: (0, h)),
            pl.BlockSpec((block_rows, 1), lambda h, b: (b, 0)),
            pl.BlockSpec((1, keys_here), lambda h, b: (0, 0)),
        ],
        out_specs=pl.BlockSpec((block_rows, HEAD), lambda h, b: (b, h)),
        out_shape=jax.ShapeDtypeStruct(query_rows.shape, query_rows.dtype),
        cost_estimate=pl.CostEstimate(
            flops=4 * shard_len * span * width,
            bytes_accessed=8 * shard_len * width,
            transcendentals=shard_len * span * width // HEAD,
        ),
        name="attend",
    )(query_rows, key_rows, value_rows, query_marks[:, None], key_marks[None, :])


def coords():
    ctx, exp = lax.axis_index("ctx"), lax.axis_index("exp")
    zh, x, y = ctx // PLANE, (ctx // NY) % NX, ctx % NY
    zl, c = exp // NC, exp % NC
    return zh * ZL + zl, x, y, c, zl


def column_weights(expert_up, expert_down, z, c):
    own = jnp.concatenate([expert_up, expert_down], axis=0)
    other = send(own, SWAP)
    ordered = jnp.where(
        c == 0, jnp.concatenate([own, other], axis=1), jnp.concatenate([other, own], axis=1)
    )
    up = jnp.zeros((NZ,) + ordered.shape[1:], ordered.dtype)
    down = jnp.zeros_like(up)

    def put(up, down, block, where):
        where = jnp.remainder(where, NZ)
        return (
            lax.dynamic_update_slice(up, block[0:1], (where, 0, 0)),
            lax.dynamic_update_slice(down, block[1:2], (where, 0, 0)),
        )

    up, down = put(up, down, ordered, z)
    sign = 1 - 2 * c
    moving = ordered
    for step in range(1, NZ // 2):
        moving = send(moving, RING)
        crossed = send(moving, SWAP)
        up, down = put(up, down, moving, z - sign * step)
        up, down = put(up, down, crossed, z + sign * step)
    half = send(lax.dynamic_slice_in_dim(moving, c, 1, 0), RING)
    crossed = send(half, SWAP)
    last = jnp.where(
        c == 0, jnp.concatenate([half, crossed], 0), jnp.concatenate([crossed, half], 0)
    )
    up, down = put(up, down, last, z + NZ // 2)
    features = up.shape[-1]
    return up.reshape(ZH, -1, features), down.reshape(ZH, -1, features)


def rotated(blocks, shift):
    n = len(blocks)
    stacked = jnp.stack(blocks + blocks)
    return lax.dynamic_slice_in_dim(stacked, jnp.remainder(-shift, n), n, 0)


def whole_projection(out_proj, x, y, c, zl):
    rows = out_proj.shape[0] // PLANE
    width = out_proj.shape[1]
    piece = lax.dynamic_slice_in_dim(out_proj, (x * NY + y) * rows, rows, 0)

    def along_z(d):
        return route(lambda z, x, y, c: (z // ZL * ZL + (z % ZL - d) % ZL, x, y, c))

    def along_y(d):
        return route(lambda z, x, y, c: (z, x, (y - d) % NY, c))

    def along_x(d):
        return route(lambda z, x, y, c: (z, (x - d) % NX, y, c))

    line = rotated([piece] + [send(piece, along_z(d)) for d in (1, 2, 3)], zl)
    line = rotated([line] + [send(line, along_y(d)) for d in (1, 2, 3)], y)
    right, left = send(line, along_x(1)), send(line, along_x(3))
    opposite = jnp.concatenate(
        [send(right[:2], along_x(1)), send(left[2:], along_x(3))], axis=0
    )
    plane = rotated([line, right, opposite, left], x)
    crossed = send(plane, SWAP)
    both = jnp.where(
        c == 0, jnp.stack([plane, crossed]), jnp.stack([crossed, plane])
    )
    return jnp.transpose(both, (3, 0, 1, 2, 4, 5)).reshape(ZL * NC, PLANE * rows, width)


def shards(
    queries,
    keys,
    values,
    segment_ids,
    out_proj,
    residual,
    norm_gain,
    expert_ids,
    gate_weights,
    expert_up,
    expert_down,
):
    z, x, y, c, zl = coords()
    shard_len = queries.shape[0]
    heads_here = queries.shape[1] // HEAD
    seg_marks = segment_ids + 1
    early_keys, early_values, early_marks = shifted((keys, values, seg_marks), "ctx", 1)
    out_whole = whole_projection(out_proj, x, y, c, zl)
    up_whole, down_whole = column_weights(expert_up, expert_down, z, c)
    attention = attend(
        queries,
        jnp.concatenate([early_keys, keys]),
        jnp.concatenate([early_values, values]),
        seg_marks,
        jnp.concatenate([early_marks, seg_marks]),
    )
    groups = lax.axis_size("exp")
    tok_rows = shard_len // groups
    mine = lax.all_to_all(
        attention.reshape(groups, tok_rows, heads_here * HEAD), "exp", 0, 0, tiled=True
    )
    projected = jnp.einsum("etk,ekd->td", mine, out_whole, preferred_element_type=jnp.float32)
    stream = (residual.astype(jnp.float32) + projected).astype(jnp.bfloat16)
    stream_f = stream.astype(jnp.float32)
    mean_square = jnp.mean(stream_f * stream_f, axis=1, keepdims=True)
    normed = (stream_f * lax.rsqrt(mean_square + 1e-06) * norm_gain[None, :]).astype(jnp.bfloat16)
    feature_count = stream.shape[1]
    experts = lax.axis_size("ctx")
    slots = experts * CAP
    flat_ids = expert_ids.reshape(-1)
    one_hot = (flat_ids[:, None] == jnp.arange(experts, dtype=jnp.int32)[None, :]).astype(jnp.int32)
    earlier = jnp.cumsum(one_hot, axis=0) - one_hot
    slot_rank = jnp.sum(earlier * one_hot, axis=1)
    place = flat_ids % PLANE * ZH + flat_ids // PLANE
    slot_grid = (place * CAP + slot_rank).reshape(tok_rows, TOP)
    hits = slot_grid[:, :, None] == jnp.arange(slots, dtype=jnp.int32)[None, None, :]
    placing = jnp.any(hits, axis=1).astype(jnp.bfloat16)
    gates = jnp.sum(jnp.where(hits, gate_weights[:, :, None], 0.0), axis=1)
    gates_high = gates.astype(jnp.bfloat16)
    gates_low = (gates - gates_high.astype(jnp.float32)).astype(jnp.bfloat16)
    outgoing = lax.dot_general(
        placing, normed, (((0,), (0,)), ((), ())), preferred_element_type=jnp.float32
    ).astype(jnp.bfloat16)
    plane_groups = [[h * PLANE + p for p in range(PLANE)] for h in range(ZH)]
    arrived = lax.all_to_all(
        outgoing.reshape(PLANE, ZH * CAP, feature_count),
        "ctx",
        0,
        0,
        axis_index_groups=plane_groups,
        tiled=True,
    )
    rows = arrived.reshape(PLANE, ZH, CAP, feature_count).transpose(1, 0, 2, 3)
    rows = rows.reshape(ZH, PLANE * CAP, feature_count)
    hidden = jax.nn.silu(
        jnp.einsum("hrd,hfd->hrf", rows, up_whole, preferred_element_type=jnp.float32)
    ).astype(jnp.bfloat16)
    result = jnp.einsum(
        "hrf,hfd->hrd", hidden, down_whole, preferred_element_type=jnp.float32
    ).astype(jnp.bfloat16)
    result = result.reshape(ZH, PLANE, CAP, feature_count).transpose(1, 0, 2, 3)
    returned = lax.all_to_all(
        result.reshape(PLANE, ZH * CAP, feature_count),
        "ctx",
        0,
        0,
        axis_index_groups=plane_groups,
        tiled=True,
    ).reshape(slots, feature_count)
    mixture = jnp.dot(gates_high, returned, preferred_element_type=jnp.float32) + jnp.dot(
        gates_low, returned, preferred_element_type=jnp.float32
    )
    return (stream_f + mixture).astype(jnp.bfloat16)


def solution(mesh):
    in_specs = (
        P("ctx", "exp"),
        P("ctx", "exp"),
        P("ctx", "exp"),
        P("ctx"),
        P("exp", None),
        P(("ctx", "exp"), None),
        P(),
        P(("ctx", "exp"), None),
        P(("ctx", "exp"), None),
        P("ctx", "exp", None),
        P("ctx", "exp", None),
    )
    out_specs = P(("ctx", "exp"), None)
    return jax.shard_map(shards, mesh=mesh, in_specs=in_specs, out_specs=out_specs, check_vma=False)
```

```python
import math
import jax
import jax.numpy as jnp
from jax import lax
from jax.experimental import pallas as pl
from jax.experimental.pallas import tpu as pltpu
from jax.sharding import PartitionSpec as P

HEAD = 128
TOP = 6
CAP = 16
MESH = pl.DeviceIdType.MESH
ZH, NX, NY, ZL, NC = 4, 4, 4, 4, 2
NZ = ZH * ZL
PLANE = NX * NY
N_CTX = ZH * PLANE


def fetch_and_attend(queries, keys, values, segment_ids, out_proj, expert_up, expert_down):
    shard_len, width = queries.shape
    block_rows = min(256, shard_len)
    span = shard_len + block_rows
    tiles = shard_len // block_rows
    scale = HEAD ** (-0.5) * math.log2(math.e)
    units, features = expert_up.shape[1:]
    rows = out_proj.shape[0] // PLANE
    last = NZ // 2

    def kernel(
        q_ref, k_ref, v_ref, mq_ref, seg_ref, proj_ref, up_ref, down_ref,
        att_ref, whole_ref, experts_ref,
        k2, v2, m2, ring_s, ring_r, swap_s, swap_r, send_s, recv_s, local_s,
    ):
        ctx, exp = lax.axis_index("ctx"), lax.axis_index("exp")
        zh, x, y = ctx // PLANE, (ctx // NY) % NX, ctx % NY
        zl, c = exp // NC, exp % NC
        z, p = zh * ZL + zl, ctx % PLANE

        def device(z, x, y, c):
            return ((z // ZL) * PLANE + x * NY + y, (z % ZL) * NC + c)

        def piece(step):
            return (z + (2 * c - 1) * step + 2 * NZ) % NZ

        partner = device(z, x, y, 1 - c)
        ahead = device((z + 1 - 2 * c + NZ) % NZ, x, y, c)
        behind = device((z + 2 * c - 1 + NZ) % NZ, x, y, c)
        line = [device(zh * ZL + (zl + d) % ZL, x, y, c) for d in (1, 2, 3)]
        column = [device(z, x, (y + d) % NY, c) for d in (1, 2, 3)]
        right, left = device(z, (x + 1) % NX, y, c), device(z, (x + 3) % NX, y, c)
        after, before = ((ctx + 1) % N_CTX, exp), ((ctx + N_CTX - 1) % N_CTX, exp)
        greeted = [partner, ahead, behind, *line, *column, right, left, after, before]
        barrier = pltpu.get_barrier_semaphore()
        for other in greeted:
            pl.semaphore_signal(barrier, inc=1, device_id=other, device_id_type=MESH)
        pl.semaphore_wait(barrier, len(greeted))

        def remote(src, dst, sent, received, target):
            return pltpu.make_async_remote_copy(
                src_ref=src, dst_ref=dst, send_sem=sent, recv_sem=received,
                device_id=target, device_id_type=MESH,
            )

        def other(src, dst, index, target):
            return remote(src, dst, send_s.at[index], recv_s.at[index], target)

        def ring_at(index, which, at):
            slot = experts_ref.at[which, at]
            return remote(slot, slot, ring_s.at[index], ring_r.at[index], ahead)

        def swap_at(index, which, at):
            slot = experts_ref.at[which, at]
            return remote(slot, slot, swap_s.at[index], swap_r.at[index], partner)

        locals_ = []
        pairs = []
        for which, ref in enumerate((up_ref, down_ref)):
            slot = experts_ref.at[which, z, c]
            pairs.append(other(ref.at[0], slot, which, partner))
            locals_.append(pltpu.make_async_copy(ref.at[0], slot, local_s.at[which]))
        for copy in pairs + locals_:
            copy.start()
        early = pl.ds(0, shard_len)
        late = pl.ds(shard_len, shard_len)
        shift = [
            other(k_ref, k2.at[early], 2, after),
            other(v_ref, v2.at[early], 3, after),
            other(seg_ref, m2.at[:, early], 4, after),
        ]
        stay = [
            pltpu.make_async_copy(k_ref, k2.at[late], local_s.at[2]),
            pltpu.make_async_copy(v_ref, v2.at[late], local_s.at[3]),
            pltpu.make_async_copy(seg_ref, m2.at[:, late], local_s.at[4]),
        ]
        rows_own = whole_ref.at[zl, c, p]
        proj_own = pltpu.make_async_copy(proj_ref.at[p], rows_own, local_s.at[5])
        along_z = [other(proj_ref.at[p], rows_own, 5 + d, line[d]) for d in range(3)]
        for copy in along_z + shift + stay + [proj_own]:
            copy.start()
        for copy in pairs:
            copy.wait()
        for copy in locals_:
            copy.wait()
        for which in range(2):
            first = ring_at(which, which, z)
            first.start()

        def service(n, step, which):
            at = piece(step)
            ring_at(n, which, at).wait_recv()
            swap_at(n, which, at).start()
            return at

        def forward(n, step, which):
            at = service(n, step, which)
            ring_at(n + 2, which, at).start()

        block_y = whole_ref.at[:, c, p]
        along_y = [other(block_y, block_y, 8 + d, column[d]) for d in range(3)]

        def x_block(at):
            return whole_ref.at[:, c, pl.ds(at * NY, NY)]

        along_x = [
            other(x_block(x), x_block(x), 11, right),
            other(x_block(x), x_block(x), 12, left),
        ]
        from_left = whole_ref.at[pl.ds(0, 2), c, pl.ds((x + 3) % NX * NY, NY)]
        from_right = whole_ref.at[pl.ds(2, 2), c, pl.ds((x + 1) % NX * NY, NY)]
        opposite = [
            other(from_left, from_left, 13, right),
            other(from_right, from_right, 14, left),
        ]
        core_half = whole_ref.at[:, c]
        crossing = other(core_half, core_half, 15, partner)

        for copy in along_z:
            copy.wait_recv()
        proj_own.wait()
        for copy in along_y:
            copy.start()
        forward(0, 1, 0)
        for copy in along_y:
            copy.wait_recv()
        for copy in along_x:
            copy.start()
        forward(1, 1, 1)
        forward(2, 2, 0)
        forward(3, 2, 1)
        for copy in stay:
            copy.wait()
        for copy in shift:
            copy.wait_recv()
        for copy in along_x:
            copy.wait_recv()
        for copy in opposite:
            copy.start()
        column_at = lax.broadcasted_iota(jnp.int32, (block_rows, span), 1)
        row_at = lax.broadcasted_iota(jnp.int32, (block_rows, span), 0)

        def one_tile(tile):
            head = pl.ds(pl.multiple_of(tile // tiles * HEAD, HEAD), HEAD)
            start = pl.multiple_of(tile % tiles * block_rows, block_rows)
            window = pl.ds(start, span)
            here = pl.ds(start, block_rows)
            scores = lax.dot_general(
                q_ref[here, head], k2[window, head], (((1,), (1,)), ((), ())),
                preferred_element_type=jnp.float32,
            )
            least = jnp.where(ctx == 0, shard_len - start, 0)
            allowed = (m2[:, window] == mq_ref[here, :]) & (column_at - row_at <= shard_len)
            allowed = allowed & (column_at >= least)
            scores = jnp.where(allowed, scores, -1e30)
            row_max = jnp.max(scores, axis=1, keepdims=True)
            weights = jnp.exp2((scores - row_max) * scale)
            total = jnp.sum(weights, axis=1, keepdims=True)
            mixed = jnp.dot(
                weights.astype(jnp.bfloat16), v2[window, head], preferred_element_type=jnp.float32
            )
            att_ref[here, head] = (mixed / total).astype(att_ref.dtype)

        per_turn = tiles * (width // HEAD) // 4

        def turn(n, carry):
            forward(n, n // 2 + 1, n % 2)

            def inner(i, carry):
                one_tile((n - 4) * per_turn + i)
                return carry

            return lax.fori_loop(0, per_turn, inner, carry)

        lax.fori_loop(4, 8, turn, 0)
        for copy in opposite:
            copy.wait_recv()
        crossing.start()
        for n in range(8, 12):
            forward(n, n // 2 + 1, n % 2)
        for which in range(2):
            service(12 + which, last - 1, which)
        ring_at(14, c, piece(last - 1)).start()
        service(14, last, c)
        for copy in along_z + along_y + along_x + opposite + shift:
            copy.wait_send()
        crossing.wait()
        for n in range(14):
            at = z
            ring_at(n, n % 2, at).wait_send()
            swap_at(n, n % 2, at).wait()
        ring_at(14, c, z).wait_send()
        swap_at(14, c, z).wait()

    anywhere = pl.BlockSpec(memory_space=pl.ANY)
    vmem = pl.BlockSpec(memory_space=pltpu.VMEM)
    return pl.pallas_call(
        kernel,
        in_specs=[vmem, anywhere, anywhere, vmem, vmem, anywhere, vmem, vmem],
        out_specs=[vmem, anywhere, anywhere],
        out_shape=[
            jax.ShapeDtypeStruct(queries.shape, queries.dtype),
            jax.ShapeDtypeStruct((ZL, NC, PLANE, rows, features), out_proj.dtype),
            jax.ShapeDtypeStruct((2, NZ, NC, units, features), expert_up.dtype),
        ],
        scratch_shapes=[
            pltpu.VMEM((2 * shard_len, width), keys.dtype),
            pltpu.VMEM((2 * shard_len, width), values.dtype),
            pltpu.VMEM((1, 2 * shard_len), jnp.int32),
            pltpu.SemaphoreType.DMA((15,)),
            pltpu.SemaphoreType.DMA((15,)),
            pltpu.SemaphoreType.DMA((15,)),
            pltpu.SemaphoreType.DMA((15,)),
            pltpu.SemaphoreType.DMA((16,)),
            pltpu.SemaphoreType.DMA((16,)),
            pltpu.SemaphoreType.DMA((6,)),
        ],
        compiler_params=pltpu.CompilerParams(
            collective_id=0, has_side_effects=True, vmem_limit_bytes=40 * 2**20
        ),
        name="fetch_and_attend",
    )(
        queries, keys, values, segment_ids[:, None], segment_ids[None, :],
        out_proj.reshape(PLANE, rows, features), expert_up, expert_down,
    )


def run_experts(arrived, experts):
    sources, count, slots, features = arrived.shape

    def kernel(x_ref, up_ref, down_ref, out_ref):
        tokens = x_ref[...].reshape(sources * slots, features)
        up = up_ref[...].reshape(-1, features)
        down = down_ref[...].reshape(-1, features)
        hidden = lax.dot_general(
            tokens, up, (((1,), (1,)), ((), ())), preferred_element_type=jnp.float32
        )
        hidden = (hidden / (1.0 + jnp.exp(-hidden))).astype(jnp.bfloat16)
        result = jnp.dot(hidden, down, preferred_element_type=jnp.float32)
        out_ref[...] = result.astype(out_ref.dtype).reshape(out_ref.shape)

    block = (sources, 1, slots, features)
    weights = (1, ZL) + experts.shape[2:]
    return pl.pallas_call(
        kernel,
        grid=(count,),
        in_specs=[
            pl.BlockSpec(block, lambda h: (0, h, 0, 0)),
            pl.BlockSpec(weights, lambda h: (0, h, 0, 0, 0)),
            pl.BlockSpec(weights, lambda h: (1, h, 0, 0, 0)),
        ],
        out_specs=pl.BlockSpec(block, lambda h: (0, h, 0, 0)),
        out_shape=jax.ShapeDtypeStruct(arrived.shape, arrived.dtype),
        name="run_experts",
    )(arrived, experts, experts)


def shards(
    queries,
    keys,
    values,
    segment_ids,
    out_proj,
    residual,
    norm_gain,
    expert_ids,
    gate_weights,
    expert_up,
    expert_down,
):
    shard_len = queries.shape[0]
    heads_here = queries.shape[1] // HEAD
    attention, out_whole, experts_here = fetch_and_attend(
        queries, keys, values, segment_ids, out_proj, expert_up, expert_down
    )
    groups = lax.axis_size("exp")
    tok_rows = shard_len // groups
    mine = lax.all_to_all(
        attention.reshape(groups, tok_rows, heads_here * HEAD), "exp", 0, 0, tiled=True
    )
    projected = jnp.einsum(
        "etk,ekd->td",
        mine,
        out_whole.reshape(groups, heads_here * HEAD, -1),
        preferred_element_type=jnp.float32,
    )
    stream = (residual.astype(jnp.float32) + projected).astype(jnp.bfloat16)
    stream_f = stream.astype(jnp.float32)
    mean_square = jnp.mean(stream_f * stream_f, axis=1, keepdims=True)
    normed = (stream_f * lax.rsqrt(mean_square + 1e-06) * norm_gain[None, :]).astype(jnp.bfloat16)
    feature_count = stream.shape[1]
    experts = lax.axis_size("ctx")
    slots = experts * CAP
    flat_ids = expert_ids.reshape(-1)
    one_hot = (flat_ids[:, None] == jnp.arange(experts, dtype=jnp.int32)[None, :]).astype(jnp.int32)
    earlier = jnp.cumsum(one_hot, axis=0) - one_hot
    slot_rank = jnp.sum(earlier * one_hot, axis=1)
    place = flat_ids % PLANE * ZH + flat_ids // PLANE
    slot_grid = (place * CAP + slot_rank).reshape(tok_rows, TOP)
    hits = slot_grid[:, :, None] == jnp.arange(slots, dtype=jnp.int32)[None, None, :]
    placing = jnp.any(hits, axis=1).astype(jnp.bfloat16)
    gates = jnp.sum(jnp.where(hits, gate_weights[:, :, None], 0.0), axis=1)
    gates_high = gates.astype(jnp.bfloat16)
    gates_low = (gates - gates_high.astype(jnp.float32)).astype(jnp.bfloat16)
    outgoing = lax.dot_general(
        placing, normed, (((0,), (0,)), ((), ())), preferred_element_type=jnp.float32
    ).astype(jnp.bfloat16)
    plane_groups = [[h * PLANE + p for p in range(PLANE)] for h in range(ZH)]
    arrived = lax.all_to_all(
        outgoing.reshape(PLANE, ZH * CAP, feature_count),
        "ctx",
        0,
        0,
        axis_index_groups=plane_groups,
        tiled=True,
    )
    result = run_experts(arrived.reshape(PLANE, ZH, CAP, feature_count), experts_here)
    returned = lax.all_to_all(
        result.reshape(PLANE, ZH * CAP, feature_count),
        "ctx",
        0,
        0,
        axis_index_groups=plane_groups,
        tiled=True,
    ).reshape(slots, feature_count)
    mixture = jnp.dot(gates_high, returned, preferred_element_type=jnp.float32) + jnp.dot(
        gates_low, returned, preferred_element_type=jnp.float32
    )
    return (stream_f + mixture).astype(jnp.bfloat16)


def solution(mesh):
    in_specs = (
        P("ctx", "exp"),
        P("ctx", "exp"),
        P("ctx", "exp"),
        P("ctx"),
        P("exp", None),
        P(("ctx", "exp"), None),
        P(),
        P(("ctx", "exp"), None),
        P(("ctx", "exp"), None),
        P("ctx", "exp", None),
        P("ctx", "exp", None),
    )
    out_specs = P(("ctx", "exp"), None)
    return jax.shard_map(shards, mesh=mesh, in_specs=in_specs, out_specs=out_specs, check_vma=False)
```

```python
import math
import jax
import jax.numpy as jnp
from jax import lax
from jax.experimental import pallas as pl
from jax.experimental.pallas import tpu as pltpu
from jax.sharding import PartitionSpec as P

HEAD = 128
TOP = 6
CAP = 16
MESH = pl.DeviceIdType.MESH
ZH, NX, NY, ZL, NC = 4, 4, 4, 4, 2
NZ = ZH * ZL
PLANE = NX * NY
N_CTX = ZH * PLANE


def place():
    ctx, exp = lax.axis_index("ctx"), lax.axis_index("exp")
    zh, x, y = ctx // PLANE, (ctx // NY) % NX, ctx % NY
    zl, c = exp // NC, exp % NC
    return zh * ZL + zl, x, y, c


def device(z, x, y, c):
    return ((z // ZL) * PLANE + x * NY + y, (z % ZL) * NC + c)


def greet(others):
    barrier = pltpu.get_barrier_semaphore()
    for other in others:
        pl.semaphore_signal(barrier, inc=1, device_id=other, device_id_type=MESH)
    pl.semaphore_wait(barrier, len(others))


def remote(src, dst, sent, received, target):
    return pltpu.make_async_remote_copy(
        src_ref=src, dst_ref=dst, send_sem=sent, recv_sem=received,
        device_id=target, device_id_type=MESH,
    )


def column_ring(experts_ref, ring_s, ring_r, swap_s, swap_r):
    z, x, y, c = place()
    partner = device(z, x, y, 1 - c)
    ahead = device((z + 1 - 2 * c + NZ) % NZ, x, y, c)
    behind = device((z + 2 * c - 1 + NZ) % NZ, x, y, c)

    def piece(step):
        return (z + (2 * c - 1) * step + 2 * NZ) % NZ

    def passing(index, which, at):
        slot = experts_ref.at[which, at]
        return remote(slot, slot, ring_s.at[index], ring_r.at[index], ahead)

    def crossing(index, which, at):
        slot = experts_ref.at[which, at]
        return remote(slot, slot, swap_s.at[index], swap_r.at[index], partner)

    return partner, ahead, behind, piece, passing, crossing


FIRST = 8


def finish_ring(experts, after):
    last = NZ // 2
    chunks = 2 * (last - 1)

    def kernel(after_ref, old_ref, experts_ref, ring_s, ring_r, swap_s, swap_r):
        c = lax.axis_index("exp") % NC
        partner, ahead, behind, piece, passing, crossing = column_ring(
            experts_ref, ring_s, ring_r, swap_s, swap_r
        )
        greet([partner, ahead, behind])
        for which in range(2):
            passing(which, which, piece(FIRST // 2)).start()
        for n in range(FIRST, chunks):
            which, at = n % 2, piece(n // 2 + 1)
            passing(n - FIRST, which, at).wait_recv()
            if n + 2 < chunks:
                passing(n + 2 - FIRST, which, at).start()
            crossing(n - FIRST, which, at).start()
        passing(chunks - FIRST, c, piece(last - 1)).start()
        passing(chunks - FIRST, c, piece(last)).wait_recv()
        crossing(chunks - FIRST, c, piece(last)).start()
        for n in range(FIRST, chunks):
            which, at = n % 2, piece(n // 2 + 1)
            passing(n - FIRST, which, at).wait_send()
            crossing(n - FIRST, which, at).wait()
        passing(chunks - FIRST, c, piece(last)).wait_send()
        crossing(chunks - FIRST, c, piece(last)).wait()

    anywhere = pl.BlockSpec(memory_space=pl.ANY)
    count = chunks + 1 - FIRST
    moved = experts.size // 2
    return pl.pallas_call(
        kernel,
        in_specs=[anywhere, anywhere],
        out_specs=anywhere,
        out_shape=jax.ShapeDtypeStruct(experts.shape, experts.dtype),
        input_output_aliases={1: 0},
        scratch_shapes=[pltpu.SemaphoreType.DMA((count,))] * 4,
        compiler_params=pltpu.CompilerParams(
            collective_id=1, has_side_effects=True, vmem_limit_bytes=8 * 2**20
        ),
        cost_estimate=pl.CostEstimate(
            flops=0, bytes_accessed=20 * moved, transcendentals=0
        ),
        name="finish_ring",
    )(after, experts)


def fetch_and_attend(queries, keys, values, segment_ids, out_proj, expert_up, expert_down):
    shard_len, width = queries.shape
    block_rows = min(256, shard_len)
    span = shard_len + block_rows
    tiles = shard_len // block_rows
    scale = HEAD ** (-0.5) * math.log2(math.e)
    units, features = expert_up.shape[1:]
    rows = out_proj.shape[0] // PLANE

    def kernel(
        q_ref, k_ref, v_ref, mq_ref, seg_ref, proj_ref, up_ref, down_ref,
        att_ref, whole_ref, experts_ref,
        k2, v2, m2, relay, ring_s, ring_r, swap_s, swap_r, send_s, recv_s, local_s,
        spread_s, spread_r, rise_s, rise_r, gather_s, gather_r,
    ):
        ctx, exp = lax.axis_index("ctx"), lax.axis_index("exp")
        zh, x, y = ctx // PLANE, (ctx // NY) % NX, ctx % NY
        zl, c = exp // NC, exp % NC
        z, p = zh * ZL + zl, ctx % PLANE

        partner, ahead, behind, piece, ring_at, swap_at = column_ring(
            experts_ref, ring_s, ring_r, swap_s, swap_r
        )
        line = [device(zh * ZL + (zl + d) % ZL, x, y, c) for d in (1, 2, 3)]
        column = [device(z, x, (y + d) % NY, c) for d in (1, 2, 3)]
        right, left = device(z, (x + 1) % NX, y, c), device(z, (x + 3) % NX, y, c)
        after, before = ((ctx + 1) % N_CTX, exp), ((ctx + N_CTX - 1) % N_CTX, exp)
        above, below = device((z + ZL) % NZ, x, y, c), device((z + NZ - ZL) % NZ, x, y, c)
        mates = [(zh * PLANE + (p + d) % PLANE, exp) for d in range(1, PLANE)]
        greet([partner, ahead, behind, *line, after, before, above, below, *mates])

        def other(src, dst, index, target):
            return remote(src, dst, send_s.at[index], recv_s.at[index], target)

        locals_ = []
        pairs = []
        for which, ref in enumerate((up_ref, down_ref)):
            slot = experts_ref.at[which, z, c]
            pairs.append(other(ref.at[0], slot, which, partner))
            locals_.append(pltpu.make_async_copy(ref.at[0], slot, local_s.at[which]))
        for copy in pairs + locals_:
            copy.start()
        early = pl.ds(0, shard_len)
        late = pl.ds(shard_len, shard_len)
        marks = other(seg_ref, m2.at[:, early], 4, after)
        shift = [other(k_ref, k2.at[early], 2, after), other(v_ref, v2.at[early], 3, after)]
        inside, final = p < PLANE - 1, p == PLANE - 1
        part = shard_len // PLANE
        both = ((k_ref, k2), (v_ref, v2))

        def spread(kv, to):
            return remote(
                both[kv][0].at[pl.ds(to * part, part)], relay.at[0, kv],
                spread_s.at[kv, to], spread_r.at[kv], (zh * PLANE + to, exp),
            )

        def rise(kv, src):
            return remote(src, relay.at[1, kv], rise_s.at[kv], rise_r.at[kv], above)

        def gather(kv, sender):
            rows_there = both[kv][1].at[pl.ds(sender * part, part)]
            return remote(
                relay.at[1, kv], rows_there,
                gather_s.at[kv], gather_r.at[kv, sender], (zh * PLANE, exp),
            )
        stay = [
            pltpu.make_async_copy(k_ref, k2.at[late], local_s.at[2]),
            pltpu.make_async_copy(v_ref, v2.at[late], local_s.at[3]),
            pltpu.make_async_copy(seg_ref, m2.at[:, late], local_s.at[4]),
        ]
        rows_own = whole_ref.at[zl, c, p]
        proj_own = pltpu.make_async_copy(proj_ref.at[p], rows_own, local_s.at[5])
        along_z = [other(proj_ref.at[p], rows_own, 5 + d, line[d]) for d in range(3)]
        for copy in along_z + stay + [marks, proj_own]:
            copy.start()

        @pl.when(inside)
        def _():
            for copy in shift:
                copy.start()

        @pl.when(final)
        def _():
            for kv in range(2):
                for to in range(PLANE - 1):
                    spread(kv, to).start()
                rise(kv, both[kv][0].at[pl.ds((PLANE - 1) * part, part)]).start()

        for copy in pairs:
            copy.wait()
        for copy in locals_:
            copy.wait()
        for which in range(2):
            first = ring_at(which, which, z)
            first.start()

        def service(n, step, which):
            at = piece(step)
            ring_at(n, which, at).wait_recv()
            swap_at(n, which, at).start()
            return at

        def forward(n, step, which):
            at = service(n, step, which)
            ring_at(n + 2, which, at).start()

        block_y = whole_ref.at[:, c, p]
        along_y = [other(block_y, block_y, 8 + d, column[d]) for d in range(3)]

        def x_block(at):
            return whole_ref.at[:, c, pl.ds(at * NY, NY)]

        along_x = [
            other(x_block(x), x_block(x), 11, right),
            other(x_block(x), x_block(x), 12, left),
        ]
        from_left = whole_ref.at[pl.ds(0, 2), c, pl.ds((x + 3) % NX * NY, NY)]
        from_right = whole_ref.at[pl.ds(2, 2), c, pl.ds((x + 1) % NX * NY, NY)]
        opposite = [
            other(from_left, from_left, 13, right),
            other(from_right, from_right, 14, left),
        ]
        core_half = whole_ref.at[:, c]
        crossing = other(core_half, core_half, 15, partner)

        for copy in along_z:
            copy.wait_recv()
        proj_own.wait()
        for copy in along_y:
            copy.start()
        forward(0, 1, 0)
        for copy in along_y:
            copy.wait_recv()
        for copy in along_x:
            copy.start()
        forward(1, 1, 1)

        @pl.when(inside)
        def _():
            for kv in range(2):
                spread(kv, 0).wait_recv()
                rise(kv, relay.at[0, kv]).start()

        forward(2, 2, 0)
        forward(3, 2, 1)
        for kv in range(2):
            rise(kv, relay.at[0, kv]).wait_recv()
        to_front = [
            pltpu.make_async_copy(
                relay.at[1, kv], both[kv][1].at[pl.ds(0, part)], local_s.at[6 + kv]
            )
            for kv in range(2)
        ]

        @pl.when(p > 0)
        def _():
            for kv in range(2):
                gather(kv, p).start()

        @pl.when(p == 0)
        def _():
            for copy in to_front:
                copy.start()

        forward(4, 3, 0)
        for copy in along_x:
            copy.wait_recv()
        for copy in opposite:
            copy.start()
        forward(5, 3, 1)
        for copy in stay:
            copy.wait()
        marks.wait_recv()

        @pl.when(p > 0)
        def _():
            for copy in shift:
                copy.wait_recv()

        @pl.when(p == 0)
        def _():
            for kv in range(2):
                to_front[kv].wait()
                for sender in range(1, PLANE):
                    gather(kv, sender).wait_recv()

        column_at = lax.broadcasted_iota(jnp.int32, (block_rows, span), 1)
        row_at = lax.broadcasted_iota(jnp.int32, (block_rows, span), 0)

        def one_tile(tile):
            head = pl.ds(pl.multiple_of(tile // tiles * HEAD, HEAD), HEAD)
            start = pl.multiple_of(tile % tiles * block_rows, block_rows)
            window = pl.ds(start, span)
            here = pl.ds(start, block_rows)
            scores = lax.dot_general(
                q_ref[here, head], k2[window, head], (((1,), (1,)), ((), ())),
                preferred_element_type=jnp.float32,
            )
            least = jnp.where(ctx == 0, shard_len - start, 0)
            allowed = (m2[:, window] == mq_ref[here, :]) & (column_at - row_at <= shard_len)
            allowed = allowed & (column_at >= least)
            scores = jnp.where(allowed, scores, -1e30)
            row_max = jnp.max(scores, axis=1, keepdims=True)
            weights = jnp.exp2((scores - row_max) * scale)
            total = jnp.sum(weights, axis=1, keepdims=True)
            mixed = jnp.dot(
                weights.astype(jnp.bfloat16), v2[window, head], preferred_element_type=jnp.float32
            )
            att_ref[here, head] = (mixed / total).astype(att_ref.dtype)

        per_turn = tiles * (width // HEAD) // 2

        def turn(n, carry):
            service(n, n // 2 + 1, n % 2)

            def inner(i, carry):
                one_tile((n - 6) * per_turn + i)
                return carry

            return lax.fori_loop(0, per_turn, inner, carry)

        for copy in opposite:
            copy.wait_recv()
        crossing.start()
        lax.fori_loop(6, FIRST, turn, 0)
        for copy in along_z + along_y + along_x + opposite + [marks]:
            copy.wait_send()
        crossing.wait()

        @pl.when(inside)
        def _():
            for kv in range(2):
                shift[kv].wait_send()
                rise(kv, relay.at[0, kv]).wait_send()

        @pl.when(final)
        def _():
            for kv in range(2):
                for to in range(PLANE - 1):
                    spread(kv, to).wait_send()
                rise(kv, both[kv][0].at[pl.ds((PLANE - 1) * part, part)]).wait_send()

        @pl.when(p > 0)
        def _():
            for kv in range(2):
                gather(kv, p).wait_send()

        for n in range(FIRST):
            ring_at(n, n % 2, z).wait_send()
            swap_at(n, n % 2, z).wait()

    anywhere = pl.BlockSpec(memory_space=pl.ANY)
    vmem = pl.BlockSpec(memory_space=pltpu.VMEM)
    return pl.pallas_call(
        kernel,
        in_specs=[vmem, anywhere, anywhere, vmem, vmem, anywhere, vmem, vmem],
        out_specs=[vmem, anywhere, anywhere],
        out_shape=[
            jax.ShapeDtypeStruct(queries.shape, queries.dtype),
            jax.ShapeDtypeStruct((ZL, NC, PLANE, rows, features), out_proj.dtype),
            jax.ShapeDtypeStruct((2, NZ, NC, units, features), expert_up.dtype),
        ],
        scratch_shapes=[
            pltpu.VMEM((2 * shard_len, width), keys.dtype),
            pltpu.VMEM((2 * shard_len, width), values.dtype),
            pltpu.VMEM((1, 2 * shard_len), jnp.int32),
            pltpu.VMEM((2, 2, shard_len // PLANE, width), keys.dtype),
            pltpu.SemaphoreType.DMA((FIRST,)),
            pltpu.SemaphoreType.DMA((FIRST,)),
            pltpu.SemaphoreType.DMA((FIRST,)),
            pltpu.SemaphoreType.DMA((FIRST,)),
            pltpu.SemaphoreType.DMA((16,)),
            pltpu.SemaphoreType.DMA((16,)),
            pltpu.SemaphoreType.DMA((8,)),
            pltpu.SemaphoreType.DMA((2, PLANE)),
            pltpu.SemaphoreType.DMA((2,)),
            pltpu.SemaphoreType.DMA((2,)),
            pltpu.SemaphoreType.DMA((2,)),
            pltpu.SemaphoreType.DMA((2,)),
            pltpu.SemaphoreType.DMA((2, PLANE)),
        ],
        compiler_params=pltpu.CompilerParams(
            collective_id=0, has_side_effects=True, vmem_limit_bytes=40 * 2**20
        ),
        name="fetch_and_attend",
    )(
        queries, keys, values, segment_ids[:, None], segment_ids[None, :],
        out_proj.reshape(PLANE, rows, features), expert_up, expert_down,
    )


def run_experts(arrived, experts):
    sources, count, slots, features = arrived.shape

    def kernel(x_ref, up_ref, down_ref, out_ref):
        tokens = x_ref[...].reshape(sources * slots, features)
        up = up_ref[...].reshape(-1, features)
        down = down_ref[...].reshape(-1, features)
        hidden = lax.dot_general(
            tokens, up, (((1,), (1,)), ((), ())), preferred_element_type=jnp.float32
        )
        hidden = (hidden / (1.0 + jnp.exp(-hidden))).astype(jnp.bfloat16)
        result = jnp.dot(hidden, down, preferred_element_type=jnp.float32)
        out_ref[...] = result.astype(out_ref.dtype).reshape(out_ref.shape)

    block = (sources, 1, slots, features)
    weights = (1, ZL) + experts.shape[2:]
    return pl.pallas_call(
        kernel,
        grid=(count,),
        in_specs=[
            pl.BlockSpec(block, lambda h: (0, h, 0, 0)),
            pl.BlockSpec(weights, lambda h: (0, h, 0, 0, 0)),
            pl.BlockSpec(weights, lambda h: (1, h, 0, 0, 0)),
        ],
        out_specs=pl.BlockSpec(block, lambda h: (0, h, 0, 0)),
        out_shape=jax.ShapeDtypeStruct(arrived.shape, arrived.dtype),
        name="run_experts",
    )(arrived, experts, experts)


def shards(
    queries,
    keys,
    values,
    segment_ids,
    out_proj,
    residual,
    norm_gain,
    expert_ids,
    gate_weights,
    expert_up,
    expert_down,
):
    shard_len = queries.shape[0]
    heads_here = queries.shape[1] // HEAD
    attention, out_whole, experts_here = fetch_and_attend(
        queries, keys, values, segment_ids, out_proj, expert_up, expert_down
    )
    groups = lax.axis_size("exp")
    tok_rows = shard_len // groups
    mine = lax.all_to_all(
        attention.reshape(groups, tok_rows, heads_here * HEAD), "exp", 0, 0, tiled=True
    )
    projected = jnp.einsum(
        "etk,ekd->td",
        mine,
        out_whole.reshape(groups, heads_here * HEAD, -1),
        preferred_element_type=jnp.float32,
    )
    stream = (residual.astype(jnp.float32) + projected).astype(jnp.bfloat16)
    stream_f = stream.astype(jnp.float32)
    mean_square = jnp.mean(stream_f * stream_f, axis=1, keepdims=True)
    normed = (stream_f * lax.rsqrt(mean_square + 1e-06) * norm_gain[None, :]).astype(jnp.bfloat16)
    feature_count = stream.shape[1]
    experts = lax.axis_size("ctx")
    slots = experts * CAP
    flat_ids = expert_ids.reshape(-1)
    one_hot = (flat_ids[:, None] == jnp.arange(experts, dtype=jnp.int32)[None, :]).astype(jnp.int32)
    earlier = jnp.cumsum(one_hot, axis=0) - one_hot
    slot_rank = jnp.sum(earlier * one_hot, axis=1)
    place = flat_ids % PLANE * ZH + flat_ids // PLANE
    slot_grid = (place * CAP + slot_rank).reshape(tok_rows, TOP)
    hits = slot_grid[:, :, None] == jnp.arange(slots, dtype=jnp.int32)[None, None, :]
    placing = jnp.any(hits, axis=1).astype(jnp.bfloat16)
    gates = jnp.sum(jnp.where(hits, gate_weights[:, :, None], 0.0), axis=1)
    gates_high = gates.astype(jnp.bfloat16)
    gates_low = (gates - gates_high.astype(jnp.float32)).astype(jnp.bfloat16)
    outgoing = lax.dot_general(
        placing, normed, (((0,), (0,)), ((), ())), preferred_element_type=jnp.float32
    ).astype(jnp.bfloat16)
    plane_groups = [[h * PLANE + p for p in range(PLANE)] for h in range(ZH)]
    arrived = lax.all_to_all(
        outgoing.reshape(PLANE, ZH * CAP, feature_count),
        "ctx",
        0,
        0,
        axis_index_groups=plane_groups,
        tiled=True,
    )
    experts_here = finish_ring(experts_here, outgoing)
    result = run_experts(arrived.reshape(PLANE, ZH, CAP, feature_count), experts_here)
    returned = lax.all_to_all(
        result.reshape(PLANE, ZH * CAP, feature_count),
        "ctx",
        0,
        0,
        axis_index_groups=plane_groups,
        tiled=True,
    ).reshape(slots, feature_count)
    mixture = jnp.dot(gates_high, returned, preferred_element_type=jnp.float32) + jnp.dot(
        gates_low, returned, preferred_element_type=jnp.float32
    )
    return (stream_f + mixture).astype(jnp.bfloat16)


def solution(mesh):
    in_specs = (
        P("ctx", "exp"),
        P("ctx", "exp"),
        P("ctx", "exp"),
        P("ctx"),
        P("exp", None),
        P(("ctx", "exp"), None),
        P(),
        P(("ctx", "exp"), None),
        P(("ctx", "exp"), None),
        P("ctx", "exp", None),
        P("ctx", "exp", None),
    )
    out_specs = P(("ctx", "exp"), None)
    return jax.shard_map(shards, mesh=mesh, in_specs=in_specs, out_specs=out_specs, check_vma=False)
```

```python
import math
import jax
import jax.numpy as jnp
from jax import lax
from jax.experimental import pallas as pl
from jax.experimental.pallas import tpu as pltpu
from jax.sharding import PartitionSpec as P

HEAD = 128
TOP = 6
CAP = 16
MESH = pl.DeviceIdType.MESH
ZH, NX, NY, ZL, NC = 4, 4, 4, 4, 2
NZ = ZH * ZL
PLANE = NX * NY
N_CTX = ZH * PLANE


def place():
    ctx, exp = lax.axis_index("ctx"), lax.axis_index("exp")
    zh, x, y = ctx // PLANE, (ctx // NY) % NX, ctx % NY
    zl, c = exp // NC, exp % NC
    return zh * ZL + zl, x, y, c


def device(z, x, y, c):
    return ((z // ZL) * PLANE + x * NY + y, (z % ZL) * NC + c)


def greet(others):
    barrier = pltpu.get_barrier_semaphore()
    for other in others:
        pl.semaphore_signal(barrier, inc=1, device_id=other, device_id_type=MESH)
    pl.semaphore_wait(barrier, len(others))


def remote(src, dst, sent, received, target):
    return pltpu.make_async_remote_copy(
        src_ref=src, dst_ref=dst, send_sem=sent, recv_sem=received,
        device_id=target, device_id_type=MESH,
    )


def column_ring(experts_ref, ring_s, ring_r, swap_s, swap_r):
    z, x, y, c = place()
    partner = device(z, x, y, 1 - c)
    ahead = device((z + 1 - 2 * c + NZ) % NZ, x, y, c)
    behind = device((z + 2 * c - 1 + NZ) % NZ, x, y, c)

    def piece(step):
        return (z + (2 * c - 1) * step + 2 * NZ) % NZ

    def passing(index, which, at):
        slot = experts_ref.at[which, at]
        return remote(slot, slot, ring_s.at[index], ring_r.at[index], ahead)

    def crossing(index, which, at):
        slot = experts_ref.at[which, at]
        return remote(slot, slot, swap_s.at[index], swap_r.at[index], partner)

    return partner, ahead, behind, piece, passing, crossing


FIRST = 10


def finish_ring(experts, after):
    last = NZ // 2
    chunks = 2 * (last - 1)

    def kernel(after_ref, old_ref, experts_ref, ring_s, ring_r, swap_s, swap_r):
        c = lax.axis_index("exp") % NC
        partner, ahead, behind, piece, passing, crossing = column_ring(
            experts_ref, ring_s, ring_r, swap_s, swap_r
        )
        greet([partner, ahead, behind])
        for which in range(2):
            passing(which, which, piece(FIRST // 2)).start()
        for n in range(FIRST, chunks):
            which, at = n % 2, piece(n // 2 + 1)
            passing(n - FIRST, which, at).wait_recv()
            if n + 2 < chunks:
                passing(n + 2 - FIRST, which, at).start()
            crossing(n - FIRST, which, at).start()
        passing(chunks - FIRST, c, piece(last - 1)).start()
        passing(chunks - FIRST, c, piece(last)).wait_recv()
        crossing(chunks - FIRST, c, piece(last)).start()
        for n in range(FIRST, chunks):
            which, at = n % 2, piece(n // 2 + 1)
            passing(n - FIRST, which, at).wait_send()
            crossing(n - FIRST, which, at).wait()
        passing(chunks - FIRST, c, piece(last)).wait_send()
        crossing(chunks - FIRST, c, piece(last)).wait()

    anywhere = pl.BlockSpec(memory_space=pl.ANY)
    count = chunks + 1 - FIRST
    moved = experts.size // 2
    return pl.pallas_call(
        kernel,
        in_specs=[anywhere, anywhere],
        out_specs=anywhere,
        out_shape=jax.ShapeDtypeStruct(experts.shape, experts.dtype),
        input_output_aliases={1: 0},
        scratch_shapes=[pltpu.SemaphoreType.DMA((count,))] * 4,
        compiler_params=pltpu.CompilerParams(
            collective_id=1, has_side_effects=True, vmem_limit_bytes=60 * 2**20
        ),
        cost_estimate=pl.CostEstimate(
            flops=0, bytes_accessed=20 * moved, transcendentals=0
        ),
        name="finish_ring",
    )(after, experts)


def fetch_and_attend(queries, keys, values, segment_ids, out_proj, expert_up, expert_down):
    shard_len, width = queries.shape
    block_rows = min(256, shard_len)
    span = shard_len + block_rows
    tiles = shard_len // block_rows
    scale = HEAD ** (-0.5) * math.log2(math.e)
    units, features = expert_up.shape[1:]
    rows = out_proj.shape[0] // PLANE

    def kernel(
        q_ref, k_ref, v_ref, mq_ref, seg_ref, proj_ref, up_ref, down_ref,
        att_ref, whole_ref, experts_ref,
        k2, v2, m2, relay, ring_s, ring_r, swap_s, swap_r, send_s, recv_s, local_s,
        spread_s, spread_r, rise_s, rise_r, gather_s, gather_r,
    ):
        ctx, exp = lax.axis_index("ctx"), lax.axis_index("exp")
        zh, x, y = ctx // PLANE, (ctx // NY) % NX, ctx % NY
        zl, c = exp // NC, exp % NC
        z, p = zh * ZL + zl, ctx % PLANE

        partner, ahead, behind, piece, ring_at, swap_at = column_ring(
            experts_ref, ring_s, ring_r, swap_s, swap_r
        )
        line = [device(zh * ZL + (zl + d) % ZL, x, y, c) for d in (1, 2, 3)]
        column = [device(z, x, (y + d) % NY, c) for d in (1, 2, 3)]
        right, left = device(z, (x + 1) % NX, y, c), device(z, (x + 3) % NX, y, c)
        after, before = ((ctx + 1) % N_CTX, exp), ((ctx + N_CTX - 1) % N_CTX, exp)
        above, below = device((z + ZL) % NZ, x, y, c), device((z + NZ - ZL) % NZ, x, y, c)
        mates = [(zh * PLANE + (p + d) % PLANE, exp) for d in range(1, PLANE)]
        greet([partner, ahead, behind, *line, after, before, above, below, *mates])

        def other(src, dst, index, target):
            return remote(src, dst, send_s.at[index], recv_s.at[index], target)

        locals_ = []
        pairs = []
        for which, ref in enumerate((up_ref, down_ref)):
            slot = experts_ref.at[which, z, c]
            pairs.append(other(ref.at[0], slot, which, partner))
            locals_.append(pltpu.make_async_copy(ref.at[0], slot, local_s.at[which]))
        for copy in pairs + locals_:
            copy.start()
        early = pl.ds(0, shard_len)
        late = pl.ds(shard_len, shard_len)
        marks = other(seg_ref, m2.at[:, early], 4, after)
        shift = [other(k_ref, k2.at[early], 2, after), other(v_ref, v2.at[early], 3, after)]
        inside, final = p < PLANE - 1, p == PLANE - 1
        part = shard_len // PLANE
        both = ((k_ref, k2), (v_ref, v2))

        def spread(kv, to):
            return remote(
                both[kv][0].at[pl.ds(to * part, part)], relay.at[0, kv],
                spread_s.at[kv, to], spread_r.at[kv], (zh * PLANE + to, exp),
            )

        def rise(kv, src):
            return remote(src, relay.at[1, kv], rise_s.at[kv], rise_r.at[kv], above)

        def gather(kv, sender):
            rows_there = both[kv][1].at[pl.ds(sender * part, part)]
            return remote(
                relay.at[1, kv], rows_there,
                gather_s.at[kv], gather_r.at[kv, sender], (zh * PLANE, exp),
            )
        stay = [
            pltpu.make_async_copy(k_ref, k2.at[late], local_s.at[2]),
            pltpu.make_async_copy(v_ref, v2.at[late], local_s.at[3]),
            pltpu.make_async_copy(seg_ref, m2.at[:, late], local_s.at[4]),
        ]
        rows_own = whole_ref.at[zl, c, p]
        proj_own = pltpu.make_async_copy(proj_ref.at[p], rows_own, local_s.at[5])
        along_z = [other(proj_ref.at[p], rows_own, 5 + d, line[d]) for d in range(3)]
        for copy in along_z + stay + [marks, proj_own]:
            copy.start()

        @pl.when(inside)
        def _():
            for copy in shift:
                copy.start()

        @pl.when(final)
        def _():
            for kv in range(2):
                for to in range(PLANE - 1):
                    spread(kv, to).start()
                rise(kv, both[kv][0].at[pl.ds((PLANE - 1) * part, part)]).start()

        for copy in pairs:
            copy.wait()
        for copy in locals_:
            copy.wait()
        for which in range(2):
            first = ring_at(which, which, z)
            first.start()

        def service(n, step, which):
            at = piece(step)
            ring_at(n, which, at).wait_recv()
            swap_at(n, which, at).start()
            return at

        def forward(n, step, which):
            at = service(n, step, which)
            ring_at(n + 2, which, at).start()

        block_y = whole_ref.at[:, c, p]
        along_y = [other(block_y, block_y, 8 + d, column[d]) for d in range(3)]

        def x_block(at):
            return whole_ref.at[:, c, pl.ds(at * NY, NY)]

        along_x = [
            other(x_block(x), x_block(x), 11, right),
            other(x_block(x), x_block(x), 12, left),
        ]
        from_left = whole_ref.at[pl.ds(0, 2), c, pl.ds((x + 3) % NX * NY, NY)]
        from_right = whole_ref.at[pl.ds(2, 2), c, pl.ds((x + 1) % NX * NY, NY)]
        opposite = [
            other(from_left, from_left, 13, right),
            other(from_right, from_right, 14, left),
        ]
        crossing = [
            other(x_block((x + d) % NX), x_block((x + d) % NX), 15 + d, partner) for d in range(NX)
        ]

        for copy in along_z:
            copy.wait_recv()
        proj_own.wait()
        for copy in along_y:
            copy.start()
        forward(0, 1, 0)
        for copy in along_y:
            copy.wait_recv()
        for copy in along_x + crossing[:1]:
            copy.start()
        forward(1, 1, 1)

        @pl.when(inside)
        def _():
            for kv in range(2):
                spread(kv, 0).wait_recv()
                rise(kv, relay.at[0, kv]).start()

        forward(2, 2, 0)
        forward(3, 2, 1)
        for kv in range(2):
            rise(kv, relay.at[0, kv]).wait_recv()
        to_front = [
            pltpu.make_async_copy(
                relay.at[1, kv], both[kv][1].at[pl.ds(0, part)], local_s.at[6 + kv]
            )
            for kv in range(2)
        ]

        @pl.when(p > 0)
        def _():
            for kv in range(2):
                gather(kv, p).start()

        @pl.when(p == 0)
        def _():
            for copy in to_front:
                copy.start()

        forward(4, 3, 0)
        for copy in along_x:
            copy.wait_recv()
        for copy in opposite + [crossing[1], crossing[3]]:
            copy.start()
        for n in range(5, FIRST - 2):
            forward(n, n // 2 + 1, n % 2)
        for copy in stay:
            copy.wait()
        marks.wait_recv()

        @pl.when(p > 0)
        def _():
            for copy in shift:
                copy.wait_recv()

        @pl.when(p == 0)
        def _():
            for kv in range(2):
                to_front[kv].wait()
                for sender in range(1, PLANE):
                    gather(kv, sender).wait_recv()

        column_at = lax.broadcasted_iota(jnp.int32, (block_rows, span), 1)
        row_at = lax.broadcasted_iota(jnp.int32, (block_rows, span), 0)

        def one_tile(tile):
            head = pl.ds(pl.multiple_of(tile // tiles * HEAD, HEAD), HEAD)
            start = pl.multiple_of(tile % tiles * block_rows, block_rows)
            window = pl.ds(start, span)
            here = pl.ds(start, block_rows)
            scores = lax.dot_general(
                q_ref[here, head], k2[window, head], (((1,), (1,)), ((), ())),
                preferred_element_type=jnp.float32,
            )
            least = jnp.where(ctx == 0, shard_len - start, 0)
            allowed = (m2[:, window] == mq_ref[here, :]) & (column_at - row_at <= shard_len)
            allowed = allowed & (column_at >= least)
            scores = jnp.where(allowed, scores, -1e30)
            row_max = jnp.max(scores, axis=1, keepdims=True)
            weights = jnp.exp2((scores - row_max) * scale)
            total = jnp.sum(weights, axis=1, keepdims=True)
            mixed = jnp.dot(
                weights.astype(jnp.bfloat16), v2[window, head], preferred_element_type=jnp.float32
            )
            att_ref[here, head] = (mixed / total).astype(att_ref.dtype)

        per_turn = tiles * (width // HEAD) // 2

        def turn(n, carry):
            service(n, n // 2 + 1, n % 2)

            def inner(i, carry):
                one_tile((n - FIRST + 2) * per_turn + i)
                return carry

            return lax.fori_loop(0, per_turn, inner, carry)

        lax.fori_loop(FIRST - 2, FIRST, turn, 0)
        for copy in opposite:
            copy.wait_recv()
        crossing[2].start()
        for copy in along_z + along_y + along_x + opposite + [marks]:
            copy.wait_send()
        for copy in crossing:
            copy.wait()

        @pl.when(inside)
        def _():
            for kv in range(2):
                shift[kv].wait_send()
                rise(kv, relay.at[0, kv]).wait_send()

        @pl.when(final)
        def _():
            for kv in range(2):
                for to in range(PLANE - 1):
                    spread(kv, to).wait_send()
                rise(kv, both[kv][0].at[pl.ds((PLANE - 1) * part, part)]).wait_send()

        @pl.when(p > 0)
        def _():
            for kv in range(2):
                gather(kv, p).wait_send()

        for n in range(FIRST):
            ring_at(n, n % 2, z).wait_send()
            swap_at(n, n % 2, z).wait()

    anywhere = pl.BlockSpec(memory_space=pl.ANY)
    vmem = pl.BlockSpec(memory_space=pltpu.VMEM)
    return pl.pallas_call(
        kernel,
        in_specs=[vmem, anywhere, anywhere, vmem, vmem, anywhere, vmem, vmem],
        out_specs=[vmem, anywhere, anywhere],
        out_shape=[
            jax.ShapeDtypeStruct(queries.shape, queries.dtype),
            jax.ShapeDtypeStruct((ZL, NC, PLANE, rows, features), out_proj.dtype),
            jax.ShapeDtypeStruct((2, NZ, NC, units, features), expert_up.dtype),
        ],
        scratch_shapes=[
            pltpu.VMEM((2 * shard_len, width), keys.dtype),
            pltpu.VMEM((2 * shard_len, width), values.dtype),
            pltpu.VMEM((1, 2 * shard_len), jnp.int32),
            pltpu.VMEM((2, 2, shard_len // PLANE, width), keys.dtype),
            pltpu.SemaphoreType.DMA((FIRST,)),
            pltpu.SemaphoreType.DMA((FIRST,)),
            pltpu.SemaphoreType.DMA((FIRST,)),
            pltpu.SemaphoreType.DMA((FIRST,)),
            pltpu.SemaphoreType.DMA((19,)),
            pltpu.SemaphoreType.DMA((19,)),
            pltpu.SemaphoreType.DMA((8,)),
            pltpu.SemaphoreType.DMA((2, PLANE)),
            pltpu.SemaphoreType.DMA((2,)),
            pltpu.SemaphoreType.DMA((2,)),
            pltpu.SemaphoreType.DMA((2,)),
            pltpu.SemaphoreType.DMA((2,)),
            pltpu.SemaphoreType.DMA((2, PLANE)),
        ],
        compiler_params=pltpu.CompilerParams(
            collective_id=0, has_side_effects=True, vmem_limit_bytes=40 * 2**20
        ),
        name="fetch_and_attend",
    )(
        queries, keys, values, segment_ids[:, None], segment_ids[None, :],
        out_proj.reshape(PLANE, rows, features), expert_up, expert_down,
    )


def run_experts(arrived, experts):
    sources, count, slots, features = arrived.shape

    def kernel(x_ref, up_ref, down_ref, out_ref):
        tokens = x_ref[...].reshape(sources * slots, features)
        up = up_ref[...].reshape(-1, features)
        down = down_ref[...].reshape(-1, features)
        hidden = lax.dot_general(
            tokens, up, (((1,), (1,)), ((), ())), preferred_element_type=jnp.float32
        )
        hidden = (hidden / (1.0 + jnp.exp(-hidden))).astype(jnp.bfloat16)
        result = jnp.dot(hidden, down, preferred_element_type=jnp.float32)
        out_ref[...] = result.astype(out_ref.dtype).reshape(out_ref.shape)

    block = (sources, 1, slots, features)
    weights = (1, ZL) + experts.shape[2:]
    return pl.pallas_call(
        kernel,
        grid=(count,),
        in_specs=[
            pl.BlockSpec(block, lambda h: (0, h, 0, 0)),
            pl.BlockSpec(weights, lambda h: (0, h, 0, 0, 0)),
            pl.BlockSpec(weights, lambda h: (1, h, 0, 0, 0)),
        ],
        out_specs=pl.BlockSpec(block, lambda h: (0, h, 0, 0)),
        out_shape=jax.ShapeDtypeStruct(arrived.shape, arrived.dtype),
        name="run_experts",
    )(arrived, experts, experts)


def shards(
    queries,
    keys,
    values,
    segment_ids,
    out_proj,
    residual,
    norm_gain,
    expert_ids,
    gate_weights,
    expert_up,
    expert_down,
):
    shard_len = queries.shape[0]
    heads_here = queries.shape[1] // HEAD
    attention, out_whole, experts_here = fetch_and_attend(
        queries, keys, values, segment_ids, out_proj, expert_up, expert_down
    )
    groups = lax.axis_size("exp")
    tok_rows = shard_len // groups
    mine = lax.all_to_all(
        attention.reshape(groups, tok_rows, heads_here * HEAD), "exp", 0, 0, tiled=True
    )
    projected = jnp.einsum(
        "etk,ekd->td",
        mine,
        out_whole.reshape(groups, heads_here * HEAD, -1),
        preferred_element_type=jnp.float32,
    )
    stream = (residual.astype(jnp.float32) + projected).astype(jnp.bfloat16)
    stream_f = stream.astype(jnp.float32)
    mean_square = jnp.mean(stream_f * stream_f, axis=1, keepdims=True)
    normed = (stream_f * lax.rsqrt(mean_square + 1e-06) * norm_gain[None, :]).astype(jnp.bfloat16)
    feature_count = stream.shape[1]
    experts = lax.axis_size("ctx")
    slots = experts * CAP
    flat_ids = expert_ids.reshape(-1)
    one_hot = (flat_ids[:, None] == jnp.arange(experts, dtype=jnp.int32)[None, :]).astype(jnp.int32)
    earlier = jnp.cumsum(one_hot, axis=0) - one_hot
    slot_rank = jnp.sum(earlier * one_hot, axis=1)
    place = flat_ids % PLANE * ZH + flat_ids // PLANE
    slot_grid = (place * CAP + slot_rank).reshape(tok_rows, TOP)
    hits = slot_grid[:, :, None] == jnp.arange(slots, dtype=jnp.int32)[None, None, :]
    placing = jnp.any(hits, axis=1).astype(jnp.bfloat16)
    gates = jnp.sum(jnp.where(hits, gate_weights[:, :, None], 0.0), axis=1)
    gates_high = gates.astype(jnp.bfloat16)
    gates_low = (gates - gates_high.astype(jnp.float32)).astype(jnp.bfloat16)
    outgoing = lax.dot_general(
        placing, normed, (((0,), (0,)), ((), ())), preferred_element_type=jnp.float32
    ).astype(jnp.bfloat16)
    plane_groups = [[h * PLANE + p for p in range(PLANE)] for h in range(ZH)]
    arrived = lax.all_to_all(
        outgoing.reshape(PLANE, ZH * CAP, feature_count),
        "ctx",
        0,
        0,
        axis_index_groups=plane_groups,
        tiled=True,
    )
    experts_here = finish_ring(experts_here, outgoing)
    result = run_experts(arrived.reshape(PLANE, ZH, CAP, feature_count), experts_here)
    returned = lax.all_to_all(
        result.reshape(PLANE, ZH * CAP, feature_count),
        "ctx",
        0,
        0,
        axis_index_groups=plane_groups,
        tiled=True,
    ).reshape(slots, feature_count)
    mixture = jnp.dot(gates_high, returned, preferred_element_type=jnp.float32) + jnp.dot(
        gates_low, returned, preferred_element_type=jnp.float32
    )
    return (stream_f + mixture).astype(jnp.bfloat16)


def solution(mesh):
    in_specs = (
        P("ctx", "exp"),
        P("ctx", "exp"),
        P("ctx", "exp"),
        P("ctx"),
        P("exp", None),
        P(("ctx", "exp"), None),
        P(),
        P(("ctx", "exp"), None),
        P(("ctx", "exp"), None),
        P("ctx", "exp", None),
        P("ctx", "exp", None),
    )
    out_specs = P(("ctx", "exp"), None)
    return jax.shard_map(shards, mesh=mesh, in_specs=in_specs, out_specs=out_specs, check_vma=False)
```
